512 devices in a mesh: mem: 16 (over z), lat: 8 (over x, y_hi), lon: 4 (over y_lo, core).
Axes of the slice: x: 4, y: 4 (y_hi: 2, y_lo: 2; y = y_hi * 2 + y_lo), z: 16, core: 2. Of those that a mesh axis runs over, the one named last changes fastest.
Arguments:
- gradient: float32 [16, 256, 1024], P('mem', 'lat', 'lon'), may hold values from -6 to 6
- perturbations: bfloat16 [80, 16, 256, 1024], P('mem', None, 'lat', 'lon'), may hold values from -6 to 6
- filter_coef: float32 [5, 256, 1024], P(None, 'lat', 'lon'), may hold values from 0.1 to 0.6
Outputs:
- hess_grad: float32 [16, 256, 1024], P('mem', 'lat', 'lon')
The draws below stay inside these ranges and needn't reach their ends.
All inputs are finite; a program needn't handle non-finite values.
Results may differ from the reference program's by a relative error of at most 0.0003.
Values may be sent and summed in bfloat16 or wider, within the bound.
No kernel may reach another device: no remote copies, remote signals or barrier semaphores. Data moves between devices by JAX's collectives and lax.ppermute only.
A program may use at most 64 MiB of HBM per device.

```python
import jax
import jax.numpy as jnp
from jax import lax

MEMBERS = 80
LEV = 16
NLAT = 256
NLON = 1024


def block_scale(own_key, dims, split, least, top_value):
    gain, own = 1.0, jax.random.fold_in(own_key, 6)
    for dim, blocks in split:
        steps = jnp.exp(jax.random.uniform(jax.random.fold_in(own, dim), (blocks,), jnp.float32, least / len(split), top_value / len(split)))
        gain = gain * jnp.repeat(steps, dims[dim] // blocks).reshape([-1 if axis == dim else 1 for axis in range(len(dims))])
    return gain


def centred(key, extent, deviation, most, split=(), kind=jnp.bfloat16):
    loudness = block_scale(key, extent, split, -0.22, 0.18) if split else 1.0
    result = jax.random.normal(key, extent, jnp.float32) * deviation * loudness
    return jnp.minimum(jnp.maximum(result, -most), most).astype(kind)


def setup_inputs(seed: int = 0) -> dict:
    key_of = jax.random.split(jax.random.key(seed), 4)
    gradient = centred(key_of[0], (LEV, NLAT, NLON), 1.0, 6.0, ((0, 16), (1, 8), (2, 4)), jnp.float32)
    perturbations = centred(key_of[1], (MEMBERS, LEV, NLAT, NLON), 1.0, 6.0, ((0, 16), (2, 8), (3, 4)))
    filter_coef = jnp.clip(0.1 + 0.5 * jax.random.uniform(key_of[2], (5, NLAT, NLON), jnp.float32) ** block_scale(key_of[2], (5, NLAT, NLON), ((1, 8), (2, 4)), -0.2, 0.2), 0.1, 0.6)
    return dict(gradient=gradient, perturbations=perturbations, filter_coef=filter_coef)


def forward_pass(values, filter_coef):
    padded = jnp.pad(values, ((0, 0), (1, 1), (1, 1)))
    out = filter_coef[0] * values + filter_coef[1] * padded[:, :-2, 1:-1]
    out = out + filter_coef[2] * padded[:, 2:, 1:-1]
    out = out + filter_coef[3] * padded[:, 1:-1, :-2]
    return out + filter_coef[4] * padded[:, 1:-1, 2:]


def adjoint_pass(values, filter_coef):
    widths = ((0, 0), (1, 1), (1, 1))
    north_term = jnp.pad(filter_coef[1] * values, widths)
    south_term = jnp.pad(filter_coef[2] * values, widths)
    west_term = jnp.pad(filter_coef[3] * values, widths)
    east_term = jnp.pad(filter_coef[4] * values, widths)
    out = filter_coef[0] * values + north_term[:, 2:, 1:-1] + south_term[:, :-2, 1:-1]
    return out + west_term[:, 1:-1, 2:] + east_term[:, 1:-1, :-2]


def reference(gradient, perturbations, filter_coef):
    def member_step(summed, member_pert):
        member_vals = member_pert.astype(jnp.float32)
        product = member_vals * gradient
        product = adjoint_pass(adjoint_pass(product, filter_coef), filter_coef)
        product = forward_pass(forward_pass(product, filter_coef), filter_coef)
        return summed + member_vals * product, None

    summed, unused = lax.scan(member_step, jnp.zeros(gradient.shape, jnp.float32), perturbations)
    return summed * (1.0 / (MEMBERS - 1))
```

```python
import jax
import jax.numpy as jnp
from jax import lax
from jax.experimental import pallas as pl
from jax.experimental.pallas import tpu as pltpu
from jax.sharding import PartitionSpec as P

MEMBERS = 80
MEM = 5
LEV = 16
ROWS = 32
COLS = 256
HALO = 4
SLOTS = ROWS + 2 * HALO
WIDE = COLS + 128
GROUPS = 2 * MEM
N_PERT = MEM * LEV
N_FIELDS = N_PERT + 2 * LEV + 2 * 5
PAIRS = N_FIELDS // 2
LANES = 512
F32, BF16 = jnp.float32, jnp.bfloat16


def parts(x):
    high = x.astype(BF16)
    return high.astype(F32), (x - high.astype(F32)).astype(BF16).astype(F32)


def own_tile(f, t, p_ref, g_ref, c_ref):
    rows = pl.ds(8 * t, 8)
    if f < N_PERT:
        return p_ref[f // LEV, f % LEV, rows, :].astype(F32)
    f -= N_PERT
    if f < 2 * LEV:
        return parts(g_ref[f % LEV, rows, :])[f // LEV]
    f -= 2 * LEV
    return parts(c_ref[f % 5, rows, :])[f // 5]


def row_kernel(p_ref, g_ref, c_ref, north_ref, south_ref):
    low = lax.broadcasted_iota(jnp.int32, (8, COLS), 0) < 4
    for q in range(PAIRS):
        a, b = (own_tile(2 * q + i, 0, p_ref, g_ref, c_ref) for i in range(2))
        north_ref[q] = jnp.where(low, a, pltpu.roll(b, 4, 0)).astype(BF16)
        a, b = (own_tile(2 * q + i, ROWS // 8 - 1, p_ref, g_ref, c_ref) for i in range(2))
        south_ref[q] = jnp.where(low, pltpu.roll(a, 4, 0), b).astype(BF16)


def halo_rows(f, from_north, from_south):
    low = lax.broadcasted_iota(jnp.int32, (8, COLS), 0) < 4
    above = from_north[f // 2].astype(F32)
    below = from_south[f // 2].astype(F32)
    if f % 2:
        above = pltpu.roll(above, 4, 0)
    else:
        below = pltpu.roll(below, 4, 0)
    return jnp.where(low, above, below)


def col_kernel(p_ref, g_ref, c_ref, from_north, from_south, west_ref, east_ref):
    lane = lax.broadcasted_iota(jnp.int32, (8, 128), 1)
    for t in range(SLOTS // 8):
        for q in range(LANES // 128):
            west = jnp.zeros((8, 128), F32)
            east = jnp.zeros((8, 128), F32)
            for k in range(32):
                f = 32 * q + k
                if f >= N_FIELDS:
                    break
                if t < ROWS // 8:
                    x = own_tile(f, t, p_ref, g_ref, c_ref)
                else:
                    x = halo_rows(f, from_north, from_south)
                mine = (lane >= 4 * k) & (lane < 4 * k + 4)
                first, last = x[:, :128], x[:, COLS - 128 :]
                if k:
                    first = pltpu.roll(first, 4 * k, 1)
                if k < 31:
                    last = pltpu.roll(last, 4 * k + 4, 1)
                west = jnp.where(mine, first, west)
                east = jnp.where(mine, last, east)
            west_ref[8 * t : 8 * t + 8, 128 * q : 128 * q + 128] = west.astype(BF16)
            east_ref[8 * t : 8 * t + 8, 128 * q : 128 * q + 128] = east.astype(BF16)


def main_kernel(
    p_ref, g_ref, c_ref, from_north, from_south, from_west, from_east, out_ref,
    a_ref, b_ref, pert_ref, grad_ref, coef_ref, sum_ref,
):
    lane = lax.broadcasted_iota(jnp.int32, (8, 128), 1)

    def side(f, t):
        q, k = f // 32, f % 32
        rows, lanes = pl.ds(8 * t, 8), slice(128 * q, 128 * q + 128)
        east = from_east[rows, lanes].astype(F32)
        west = from_west[rows, lanes].astype(F32)
        if k:
            east = pltpu.roll(east, 128 - 4 * k, 1)
        if k < 31:
            west = pltpu.roll(west, 124 - 4 * k, 1)
        return jnp.where(lane < 4, east, jnp.where(lane >= 124, west, 0.0))

    def coef_tile(k, t):
        f = N_PERT + 2 * LEV + k
        if isinstance(t, int) and t == ROWS // 8:
            body = halo_rows(f, from_north, from_south) + halo_rows(f + 5, from_north, from_south)
        else:
            body = c_ref[k, pl.ds(8 * t, 8), :]
        return jnp.concatenate([body, side(f, t) + side(f + 5, t)], axis=1)

    def grad_tile(level, t):
        f = N_PERT + level
        if isinstance(t, int) and t == ROWS // 8:
            body = halo_rows(f, from_north, from_south)
            body = body + halo_rows(f + LEV, from_north, from_south)
        else:
            body = g_ref[level, pl.ds(8 * t, 8), :]
        return jnp.concatenate([body, side(f, t) + side(f + LEV, t)], axis=1)

    def pert_tile(m, level, t):
        f = m * LEV + level
        if isinstance(t, int) and t == ROWS // 8:
            body = halo_rows(f, from_north, from_south)
        else:
            body = p_ref[m, level, pl.ds(8 * t, 8), :].astype(F32)
        return jnp.concatenate([body, side(f, t)], axis=1)

    def slot(t, s):
        if isinstance(t, int) and t == ROWS // 8:
            return s if s < HALO else ROWS + s
        return HALO + 8 * t + s

    def unpack(t):
        for k in range(5):
            tile = coef_tile(k, t)
            for s in range(8):
                coef_ref[k, slot(t, s)] = jnp.broadcast_to(tile[s : s + 1], (8, WIDE))
        for half in range(2):
            tile = jnp.stack([grad_tile(8 * half + j, t) for j in range(8)])
            tile = jnp.swapaxes(tile, 0, 1)
            for s in range(8):
                grad_ref[slot(t, s), half] = tile[s]
        for m in range(MEM):
            for half in range(2):
                tile = jnp.stack([pert_tile(m, 8 * half + j, t) for j in range(8)])
                tile = jnp.swapaxes(tile, 0, 1)
                for s in range(8):
                    if not isinstance(t, int):
                        pert_ref[8 * t + s, 2 * m + half] = tile[s, :, :COLS]
                    a_ref[slot(t, s), 2 * m + half] = tile[s] * grad_ref[slot(t, s), half]

    lax.fori_loop(0, ROWS // 8, lambda t, c: (unpack(t), c)[1], 0)
    unpack(ROWS // 8)

    def turned(r, carry):
        inside = coef_ref[0, r] > 0.0
        coef_ref[5, r] = jnp.where(inside, coef_ref[1, r + 1], 0.0)
        coef_ref[6, r] = jnp.where(inside, coef_ref[2, r - 1], 0.0)
        coef_ref[7, r] = jnp.where(inside, pltpu.roll(coef_ref[3, r], WIDE - 1, 1), 0.0)
        coef_ref[8, r] = jnp.where(inside, pltpu.roll(coef_ref[4, r], 1, 1), 0.0)
        return carry

    lax.fori_loop(1, SLOTS - 1, turned, 0)

    def stencil(src, r, n, centre, above, below, left, right, width):
        x = src[r, n]
        out = centre * x[:, :width] + above * src[r - 1, n, :, :width]
        out = out + below * src[r + 1, n, :, :width]
        out = out + left * pltpu.roll(x, 1, 1)[:, :width]
        return out + right * pltpu.roll(x, WIDE - 1, 1)[:, :width]

    def adjoint(src, dst, margin):
        def row(r, carry):
            coefs = [coef_ref[k, r] for k in (0, 6, 5, 8, 7)]
            for n in range(GROUPS):
                dst[r, n] = stencil(src, r, n, *coefs, WIDE)
            return carry

        lax.fori_loop(HALO - margin, ROWS + HALO + margin, row, 0)

    def forward(src, dst, margin):
        def row(r, carry):
            coefs = [coef_ref[k, r] for k in range(5)]
            for n in range(GROUPS):
                dst[r, n] = stencil(src, r, n, *coefs, WIDE)
            return carry

        lax.fori_loop(HALO - margin, ROWS + HALO + margin, row, 0)

    def last(src):
        def row(r, carry):
            coefs = [coef_ref[k, r, :, :COLS] for k in range(5)]
            for half in range(2):
                total = None
                for m in range(MEM):
                    n = 2 * m + half
                    term = pert_ref[r - HALO, n] * stencil(src, r, n, *coefs, COLS)
                    total = term if total is None else total + term
                sum_ref[r - HALO, half] = total * (1.0 / (MEMBERS - 1))
            return carry

        lax.fori_loop(HALO, ROWS + HALO, row, 0)

    adjoint(a_ref, b_ref, 3)
    adjoint(b_ref, a_ref, 2)
    forward(a_ref, b_ref, 1)
    last(b_ref)

    for half in range(2):
        for t in range(ROWS // 8):
            tile = jnp.stack([sum_ref[8 * t + s, half] for s in range(8)])
            tile = jnp.swapaxes(tile, 0, 1)
            for j in range(8):
                out_ref[8 * half + j, 8 * t : 8 * t + 8, :] = tile[j]


VMEM = pl.BlockSpec(memory_space=pltpu.VMEM)


def call(kernel, outs, scratch=()):
    def run(*args):
        return pl.pallas_call(
            kernel,
            out_shape=outs,
            in_specs=[VMEM] * len(args),
            out_specs=jax.tree.map(lambda _: VMEM, outs),
            scratch_shapes=list(scratch),
        )(*args)

    return run


def neighbours(axis):
    count = lax.axis_size(axis)
    forward = [(i, i + 1) for i in range(count - 1)]
    return forward, [(target, source) for source, target in forward]


def body(gradient, perturbations, filter_coef):
    grad = lax.all_gather(gradient, "mem", axis=0, tiled=True)
    shape = jax.ShapeDtypeStruct
    rows = shape((PAIRS, 8, COLS), BF16)
    to_north, to_south = call(row_kernel, [rows, rows])(perturbations, grad, filter_coef)
    forward, backward = neighbours("lat")
    from_north = lax.ppermute(to_south, "lat", forward)
    from_south = lax.ppermute(to_north, "lat", backward)
    own = (perturbations, grad, filter_coef, from_north, from_south)
    cols = shape((SLOTS, LANES), BF16)
    to_west, to_east = call(col_kernel, [cols, cols])(*own)
    forward, backward = neighbours("lon")
    from_west = lax.ppermute(to_east, "lon", forward)
    from_east = lax.ppermute(to_west, "lon", backward)
    part = call(
        main_kernel,
        shape((LEV, ROWS, COLS), F32),
        [
            pltpu.VMEM((SLOTS, GROUPS, 8, WIDE), F32),
            pltpu.VMEM((SLOTS, GROUPS, 8, WIDE), F32),
            pltpu.VMEM((ROWS, GROUPS, 8, COLS), F32),
            pltpu.VMEM((SLOTS, 2, 8, WIDE), F32),
            pltpu.VMEM((9, SLOTS, 8, WIDE), F32),
            pltpu.VMEM((ROWS, 2, 8, COLS), F32),
        ],
    )(*own, from_west, from_east)
    part = lax.all_to_all(part, "mem", split_axis=0, concat_axis=0, tiled=True)
    return jnp.sum(part, axis=0, keepdims=True)


def solution(mesh):
    return jax.shard_map(
        body,
        mesh=mesh,
        in_specs=(P("mem", "lat", "lon"), P("mem", None, "lat", "lon"), P(None, "lat", "lon")),
        out_specs=P("mem", "lat", "lon"),
        check_vma=False,
    )
```

```python
import jax
import jax.numpy as jnp
import numpy as np
from jax import lax
from jax.experimental import pallas as pl
from jax.experimental.pallas import tpu as pltpu
from jax.sharding import PartitionSpec as P


MEMBERS = 80
GROUPS = MEMBERS // 8
PACK = 5
PACKS = GROUPS // PACK
ROWS = 32
COLS = 256
HALO = 4
SLOTS = ROWS + 2 * HALO
EDGE = 24
WIDE = COLS + 128
GRAD, PLANES = 9, 10
SIDE = MEMBERS * HALO
F32, BF16 = jnp.float32, jnp.bfloat16


def one_hot(depth, width, pairs):
    table = np.zeros((depth, width), np.float32)
    for source, target in pairs:
        table[source, target] = 1.0
    return table.astype(BF16)


def split_pairs(first=0):
    return [(first + c, c // 2 + 128 * (c % 2)) for c in range(COLS)]


def tables():
    every = range(PACK)
    send, edges, spread, back = [], [], [], []
    for i in every:
        at = EDGE * i
        west = [(c, at + 20 + c) for c in range(4)]
        send.append(one_hot(COLS, 256, west + [(252 + c, 128 + at + c) for c in range(4)]))
        west = [(c, at + 4 + c) for c in range(8)]
        edges.append(one_hot(COLS, 128, west + [(COLS - 8 + c, at + 12 + c) for c in range(8)]))
        spread += [(c, COLS + at + c) for c in range(12)]
        spread += [(COLS - 16 + c, COLS + at + c) for c in range(12, 24)]
        back += [(at + 4 + c, c // 2 + 128 * (c % 2)) for c in range(4)]
        back += [(at + 16 + c, 126 + c // 2 + 128 * (c % 2)) for c in range(4)]
    planes = one_hot(COLS + 2 * HALO, WIDE, split_pairs(HALO) + spread)
    join = one_hot(COLS, COLS, [(target, source) for source, target in split_pairs()])
    split = one_hot(COLS, COLS, split_pairs())
    return np.stack(send), np.stack(edges), planes, split, one_hot(128, COLS, back), join


def parts(x, count=3):
    out = []
    for _ in range(count):
        out.append(x.astype(BF16))
        x = x - out[-1].astype(F32)
    return out


def dot(a, b):
    return jnp.dot(a, b, preferred_element_type=F32)


def moved(x, table):
    first, second, third = (dot(y, table) for y in parts(x))
    return (third + second) + first


def planes_kernel(x_ref, table, out_ref, rows_ref):
    for k in range(6):
        x = moved(x_ref[k], table[...])
        for i in range(WIDE // 128):
            lanes = slice(128 * i, 128 * i + 128)
            out_ref[(GRAD if k == 5 else k), i] = x[:, lanes]
            rows_ref[k, 8 : 8 + SLOTS, lanes] = x[:, lanes]
    inside = rows_ref[0, 8 : 8 + SLOTS, :] > 0.0
    below = rows_ref[1, 9 : 9 + SLOTS, :]
    above = rows_ref[2, 7 : 7 + SLOTS, :]
    right = both(rows_ref[3, 8 : 8 + SLOTS, :])[1]
    left = both(rows_ref[4, 8 : 8 + SLOTS, :])[0]
    for k, x in enumerate((below, above, right, left)):
        x = jnp.where(inside, x, 0.0)
        for i in range(WIDE // 128):
            out_ref[5 + k, i] = x[:, 128 * i : 128 * i + 128]


def shifted(even, odd):
    left = (pltpu.roll(odd, 1, 1), even)
    right = (odd, pltpu.roll(even, 127, 1))
    return left, right


def shifted_edge(x):
    return pltpu.roll(x, 1, 1), pltpu.roll(x, 127, 1)


def both(x):
    left, right = shifted(x[:, :128], x[:, 128:256])
    edge_left, edge_right = shifted_edge(x[:, 256:])
    return jnp.concatenate([*left, edge_left], 1), jnp.concatenate([*right, edge_right], 1)


def row_kernel(top, bottom, north_ref, south_ref):
    low = lax.broadcasted_iota(jnp.int32, (8, COLS), 0) < HALO
    for q in range(0, MEMBERS, 4):
        x = [top[q + i].astype(F32) for i in range(4)]
        x = [jnp.where(low, x[i], pltpu.roll(x[i + 1], 4, 0)) for i in (0, 2)]
        north_ref[4 * q : 4 * q + 16, :] = jnp.concatenate(x, axis=0).astype(BF16)
        x = [bottom[q + i].astype(F32) for i in range(4)]
        x = [jnp.where(low, pltpu.roll(x[i], 4, 0), x[i + 1]) for i in (0, 2)]
        south_ref[4 * q : 4 * q + 16, :] = jnp.concatenate(x, axis=0).astype(BF16)


def pack_rows(ref, pack, i):
    size = 8 * HALO
    return ref[pl.ds((PACK * pack + i) * size, size), :]


def group_rows(ref, pack, i):
    return ref[pl.ds(8 * (PACK * pack + i), 8)].reshape(8 * ROWS, COLS)


def col_kernel(p_ref, from_north, from_south, send, west_ref, east_ref):
    own, side = 8 * ROWS, 8 * HALO
    for pack in range(PACKS):
        at = pack * (own + 2 * side)
        for rows, get in (
            (own, lambda i: group_rows(p_ref, pack, i)),
            (side, lambda i: pack_rows(from_north, pack, i)),
            (side, lambda i: pack_rows(from_south, pack, i)),
        ):
            x = dot(get(0), send[0])
            for i in range(1, PACK):
                x = x + dot(get(i), send[i])
            west_ref[at : at + rows, :] = x[:, :128].astype(BF16)
            east_ref[at : at + rows, :] = x[:, 128:].astype(BF16)
            at += rows


def main_kernel(
    p_ref, planes, from_north, from_south, from_west, from_east, edges, split, back, join, out_ref,
    a_ref, b_ref, a_edge, b_edge, pert_ref, pert_edge, sum_ref, sum_edge,
):
    def halves(north, south):
        low = lax.broadcasted_iota(jnp.int32, (8, north.shape[1]), 0) < HALO
        tiles = []
        for q in range(north.shape[0] // 8):
            n, s = north[8 * q : 8 * q + 8], south[8 * q : 8 * q + 8]
            tiles.append(jnp.where(low, n, pltpu.roll(s, 4, 0)))
            tiles.append(jnp.where(low, pltpu.roll(n, 4, 0), s))
        return jnp.stack(tiles)

    def turn(tile):
        return jnp.swapaxes(tile, 0, 1)

    def halo_slot(s):
        return s if s < HALO else ROWS + s

    def plane(k, r, tiles):
        return [planes[k, i, pl.ds(r, 8, stride=0), :] for i in tiles]

    def wide(k, r):
        return jnp.concatenate(plane(k, r, (0, 1)), axis=1)

    own, side = 8 * ROWS, 8 * HALO
    for pack in range(PACKS):
        at = pack * (own + 2 * side)

        def received(start, rows):
            return from_east[start : start + rows, :].astype(F32) + from_west[
                start : start + rows, :
            ].astype(F32)

        x = received(at, own)
        for i in range(PACK):
            x = x + dot(group_rows(p_ref, pack, i), edges[i])
        x = x.reshape(8, ROWS, 128)
        for t in range(ROWS // 8):
            tile = turn(x[:, 8 * t : 8 * t + 8])
            for s in range(8):
                r = HALO + 8 * t + s
                pert_edge[8 * t + s, pack] = tile[s]
                a_edge[r, pack] = tile[s] * plane(GRAD, r, (2,))[0]
        x = [received(at + own + j * side, side) for j in range(2)]
        for j, src in enumerate((from_north, from_south)):
            for i in range(PACK):
                x[j] = x[j] + dot(pack_rows(src, pack, i), edges[i])
        tile = turn(halves(*x))
        for s in range(8):
            r = halo_slot(s)
            a_edge[r, pack] = tile[s] * plane(GRAD, r, (2,))[0]

    def products(n, carry):
        x = dot(p_ref[pl.ds(8 * n, 8)].reshape(own, COLS), split[...]).reshape(8, ROWS, COLS)
        for t in range(ROWS // 8):
            tile = turn(x[:, 8 * t : 8 * t + 8])
            for s in range(8):
                r = HALO + 8 * t + s
                pert_ref[8 * t + s, n] = tile[s]
                a_ref[r, n] = tile[s] * wide(GRAD, r)
        here = pl.ds(pl.multiple_of(n * side, side), side)
        tile = turn(halves(*(dot(x[here, :], split[...]) for x in (from_north, from_south))))
        for s in range(8):
            r = halo_slot(s)
            a_ref[r, n] = tile[s] * wide(GRAD, r)
        return carry

    lax.fori_loop(0, GROUPS, products, 0)

    def weighted(coefs, x, above, below, left, right):
        out = coefs[0] * x + coefs[1] * above
        out = out + coefs[2] * below
        return (out + coefs[3] * left) + coefs[4] * right

    def stencil(ref, r, n, coefs):
        x = [ref[r, n, :, 128 * i : 128 * i + 128] for i in range(2)]
        left, right = shifted(*x)
        return [
            weighted(
                [c[i] for c in coefs],
                x[i],
                ref[r - 1, n, :, 128 * i : 128 * i + 128],
                ref[r + 1, n, :, 128 * i : 128 * i + 128],
                left[i],
                right[i],
            )
            for i in range(2)
        ]

    def stencil_edge(ref, r, n, coefs):
        x = ref[r, n]
        return weighted([c[2] for c in coefs], x, ref[r - 1, n], ref[r + 1, n], *shifted_edge(x))

    STEP = 2

    def each_row(margin, order, use):
        def step(i, carry):
            for d in range(STEP):
                r = HALO - margin + STEP * i + d
                use(r, [plane(k, r, range(3)) for k in order])
            return carry

        lax.fori_loop(0, (ROWS + 2 * margin) // STEP, step, 0)

    def filter_pass(src, src_edge, dst, dst_edge, margin, order):
        def use(r, coefs):
            for n in range(GROUPS):
                for i, x in enumerate(stencil(src, r, n, coefs)):
                    dst[r, n, :, 128 * i : 128 * i + 128] = x
            for pack in range(PACKS):
                dst_edge[r, pack] = stencil_edge(src_edge, r, pack, coefs)

        each_row(margin, order, use)

    adjoint, forward = (0, 6, 5, 8, 7), range(5)
    filter_pass(a_ref, a_edge, b_ref, b_edge, 3, adjoint)
    filter_pass(b_ref, b_edge, a_ref, a_edge, 2, adjoint)
    filter_pass(a_ref, a_edge, b_ref, b_edge, 1, forward)

    def last(r, coefs):
        total = [None, None]
        for n in range(GROUPS):
            for i, x in enumerate(stencil(b_ref, r, n, coefs)):
                x = pert_ref[r - HALO, n, :, 128 * i : 128 * i + 128] * x
                total[i] = x if total[i] is None else total[i] + x
        for i in range(2):
            sum_ref[r - HALO, :, 128 * i : 128 * i + 128] = total[i]
        total = None
        for pack in range(PACKS):
            x = pert_edge[r - HALO, pack] * stencil_edge(b_edge, r, pack, coefs)
            total = x if total is None else total + x
        sum_edge[r - HALO] = total

    each_row(0, forward, last)

    def members(ref):
        x = jnp.swapaxes(ref[...], 0, 1)
        total = x[0]
        for j in range(1, 8):
            total = total + x[j]
        return total

    lane = lax.broadcasted_iota(jnp.int32, (ROWS, COLS), 1) % 128
    edge = moved(members(sum_edge), back[...])
    total = jnp.where((lane >= 2) & (lane < 126), members(sum_ref), edge)
    out_ref[0] = moved(total, join[...]) * (1.0 / (MEMBERS - 1))


VMEM = pl.BlockSpec(memory_space=pltpu.VMEM)


def call(kernel, outs, scratch=()):
    def run(*args):
        return pl.pallas_call(
            kernel,
            out_shape=outs,
            in_specs=[VMEM] * len(args),
            out_specs=jax.tree.map(lambda _: VMEM, outs),
            scratch_shapes=list(scratch),
        )(*args)

    return run


def row_messages(pert):
    out = jax.ShapeDtypeStruct((SIDE, COLS), BF16)
    shape = (MEMBERS, 8, COLS)
    return pl.pallas_call(
        row_kernel,
        grid=(1,),
        in_specs=[
            pl.BlockSpec(shape, lambda i: (0, 0, 0)),
            pl.BlockSpec(shape, lambda i: (0, ROWS // 8 - 1, 0)),
        ],
        out_specs=[pl.BlockSpec((SIDE, COLS), lambda i: (0, 0))] * 2,
        out_shape=[out, out],
    )(pert, pert)


def swap(to_low, to_high, axis):
    count = lax.axis_size(axis)
    forward = [(i, i + 1) for i in range(count - 1)]
    backward = [(target, source) for source, target in forward]
    return lax.ppermute(to_high, axis, forward), lax.ppermute(to_low, axis, backward)


def extended(block):
    low, high = swap(block[:, :HALO], block[:, -HALO:], "lat")
    block = jnp.concatenate([low, block, high], axis=1)
    low, high = swap(block[:, :, :HALO], block[:, :, -HALO:], "lon")
    return jnp.concatenate([low, block, high], axis=2)


def body(gradient, perturbations, filter_coef):
    send, edges, spread, split, back, join = tables()
    shape = jax.ShapeDtypeStruct
    pert = lax.all_to_all(perturbations, "mem", split_axis=1, concat_axis=0, tiled=True)
    pert = pert.reshape(MEMBERS, ROWS, COLS)
    planes = call(
        planes_kernel,
        shape((PLANES, WIDE // 128, SLOTS, 128), F32),
        [pltpu.VMEM((6, SLOTS + 16, WIDE), F32)],
    )(extended(jnp.concatenate([filter_coef, gradient], axis=0)), spread)
    from_north, from_south = swap(*row_messages(pert), "lat")
    cols = shape((MEMBERS * SLOTS // PACK, 128), BF16)
    to_west, to_east = call(col_kernel, [cols, cols])(pert, from_north, from_south, send)
    from_west, from_east = swap(to_west, to_east, "lon")
    return call(
        main_kernel,
        shape((1, ROWS, COLS), F32),
        [
            pltpu.VMEM((SLOTS, GROUPS, 8, COLS), F32),
            pltpu.VMEM((SLOTS, GROUPS, 8, COLS), F32),
            pltpu.VMEM((SLOTS, PACKS, 8, 128), F32),
            pltpu.VMEM((SLOTS, PACKS, 8, 128), F32),
            pltpu.VMEM((ROWS, GROUPS, 8, COLS), F32),
            pltpu.VMEM((ROWS, PACKS, 8, 128), F32),
            pltpu.VMEM((ROWS, 8, COLS), F32),
            pltpu.VMEM((ROWS, 8, 128), F32),
        ],
    )(pert, planes, from_north, from_south, from_west, from_east, edges, split, back, join)


def solution(mesh):
    return jax.shard_map(
        body,
        mesh=mesh,
        in_specs=(P("mem", "lat", "lon"), P("mem", None, "lat", "lon"), P(None, "lat", "lon")),
        out_specs=P("mem", "lat", "lon"),
        check_vma=False,
    )
```

```python
import jax
import jax.numpy as jnp
import numpy as np
from jax import lax
from jax.experimental import pallas as pl
from jax.experimental.pallas import tpu as pltpu
from jax.sharding import PartitionSpec as P


MEMBERS = 80
GROUPS = MEMBERS // 8
PACK = 5
PACKS = GROUPS // PACK
ROWS = 32
COLS = 256
HALO = 4
SLOTS = ROWS + 2 * HALO
EDGE = 24
WIDE = COLS + 128
GRAD, PLANES = 9, 10
SIDE = MEMBERS * HALO
F32, BF16 = jnp.float32, jnp.bfloat16


def one_hot(depth, width, pairs):
    table = np.zeros((depth, width), np.float32)
    for source, target in pairs:
        table[source, target] = 1.0
    return table.astype(BF16)


def split_pairs(first=0):
    return [(first + c, c // 2 + 128 * (c % 2)) for c in range(COLS)]


def tables():
    spread, back = [], []
    for i in range(PACK):
        at = EDGE * i
        spread += [(c, COLS + at + c) for c in range(12)]
        spread += [(COLS - 16 + c, COLS + at + c) for c in range(12, 24)]
        back += [(at + 4 + c, c // 2 + 128 * (c % 2)) for c in range(4)]
        back += [(at + 16 + c, 126 + c // 2 + 128 * (c % 2)) for c in range(4)]
    planes = one_hot(COLS + 2 * HALO, WIDE, split_pairs(HALO) + spread)
    join = one_hot(COLS, COLS, [(target, source) for source, target in split_pairs()])
    split = one_hot(COLS, COLS, split_pairs())
    return planes, split, one_hot(128, COLS, back), join


def edge_table(width, first, last, count):
    def ends(shift, keep):
        row = lax.broadcasted_iota(jnp.int32, (16, width), 0)
        lane = lax.broadcasted_iota(jnp.int32, (16, width), 1)
        return jnp.where((lane - row == shift) & keep(row), 1.0, 0.0).astype(BF16)

    top = ends(first, lambda row: row < count)
    bottom = ends(last + count - 16, lambda row: row >= 16 - count)
    return jnp.concatenate([top, jnp.zeros((COLS - 32, width), BF16), bottom], axis=0)


def send_table(i):
    return edge_table(256, EDGE * i + 20, 128 + EDGE * i, 4)


def own_table(i):
    return edge_table(128, EDGE * i + 4, EDGE * i + 12, 8)


def parts(x, count=3):
    out = []
    for _ in range(count):
        out.append(x.astype(BF16))
        x = x - out[-1].astype(F32)
    return out


def dot(a, b):
    return jnp.dot(a, b, preferred_element_type=F32)


def moved(x, table):
    first, second, third = (dot(y, table) for y in parts(x))
    return (third + second) + first


def planes_kernel(x_ref, table, out_ref, rows_ref):
    for k in range(6):
        x = moved(x_ref[k], table[...])
        for i in range(WIDE // 128):
            lanes = slice(128 * i, 128 * i + 128)
            out_ref[(GRAD if k == 5 else k), i] = x[:, lanes]
            rows_ref[k, 8 : 8 + SLOTS, lanes] = x[:, lanes]
    inside = rows_ref[0, 8 : 8 + SLOTS, :] > 0.0
    below = rows_ref[1, 9 : 9 + SLOTS, :]
    above = rows_ref[2, 7 : 7 + SLOTS, :]
    right = both(rows_ref[3, 8 : 8 + SLOTS, :])[1]
    left = both(rows_ref[4, 8 : 8 + SLOTS, :])[0]
    for k, x in enumerate((below, above, right, left)):
        x = jnp.where(inside, x, 0.0)
        for i in range(WIDE // 128):
            out_ref[5 + k, i] = x[:, 128 * i : 128 * i + 128]


def shifted(even, odd):
    left = (pltpu.roll(odd, 1, 1), even)
    right = (odd, pltpu.roll(even, 127, 1))
    return left, right


def shifted_edge(x):
    return pltpu.roll(x, 1, 1), pltpu.roll(x, 127, 1)


def both(x):
    left, right = shifted(x[:, :128], x[:, 128:256])
    edge_left, edge_right = shifted_edge(x[:, 256:])
    return jnp.concatenate([*left, edge_left], 1), jnp.concatenate([*right, edge_right], 1)


def row_kernel(p_ref, north_ref, south_ref):
    low = lax.broadcasted_iota(jnp.int32, (8, COLS), 0) < HALO
    for q in range(0, MEMBERS, 4):
        x = [p_ref[q + i, :8].astype(F32) for i in range(4)]
        x = [jnp.where(low, x[i], pltpu.roll(x[i + 1], 4, 0)) for i in (0, 2)]
        north_ref[4 * q : 4 * q + 16, :] = jnp.concatenate(x, axis=0).astype(BF16)
        x = [p_ref[q + i, ROWS - 8 :].astype(F32) for i in range(4)]
        x = [jnp.where(low, pltpu.roll(x[i], 4, 0), x[i + 1]) for i in (0, 2)]
        south_ref[4 * q : 4 * q + 16, :] = jnp.concatenate(x, axis=0).astype(BF16)


def pack_rows(ref, pack, i):
    size = 8 * HALO
    return ref[pl.ds((PACK * pack + i) * size, size), :]


def group_rows(ref, pack, i):
    return ref[pl.ds(8 * (PACK * pack + i), 8)].reshape(8 * ROWS, COLS)


def col_kernel(p_ref, from_north, from_south, west_ref, east_ref):
    send = [send_table(i) for i in range(PACK)]
    own, side = 8 * ROWS, 8 * HALO
    edges = [own_table(i) for i in range(PACK)]
    for pack in range(PACKS):
        at = pack * (own + 2 * side)
        for rows, get in (
            (own, lambda i: group_rows(p_ref, pack, i)),
            (side, lambda i: pack_rows(from_north, pack, i)),
            (side, lambda i: pack_rows(from_south, pack, i)),
        ):
            x = dot(get(0), send[0])
            for i in range(1, PACK):
                x = x + dot(get(i), send[i])
            west_ref[at : at + rows, :] = x[:, :128].astype(BF16)
            east_ref[at : at + rows, :] = x[:, 128:].astype(BF16)
            at += rows


def turn(tile):
    return jnp.swapaxes(tile, 0, 1)


def turn_kernel(p_ref, split, out_ref):
    def group(n, carry):
        x = p_ref[pl.ds(pl.multiple_of(8 * n, 8), 8)].reshape(8 * ROWS, COLS)
        x = dot(x, split[...]).reshape(8, ROWS, COLS)
        for t in range(ROWS // 8):
            tile = turn(x[:, 8 * t : 8 * t + 8])
            for s in range(8):
                out_ref[n, 8 * t + s] = tile[s]
        return carry

    lax.fori_loop(0, GROUPS, group, 0)


def main_kernel(
    p_ref, turned, planes, from_north, from_south, from_west, from_east, split, back, join, out_ref,
    a_ref, b_ref, a_edge, b_edge, pert_ref, pert_edge, sum_ref, sum_edge, sems,
):
    copies = [
        pltpu.make_async_copy(turned.at[n], pert_ref.at[n], sems.at[n]) for n in range(GROUPS)
    ]
    for copy in copies:
        copy.start()

    def halves(north, south):
        low = lax.broadcasted_iota(jnp.int32, (8, north.shape[1]), 0) < HALO
        tiles = []
        for q in range(north.shape[0] // 8):
            n, s = north[8 * q : 8 * q + 8], south[8 * q : 8 * q + 8]
            tiles.append(jnp.where(low, n, pltpu.roll(s, 4, 0)))
            tiles.append(jnp.where(low, pltpu.roll(n, 4, 0), s))
        return jnp.stack(tiles)

    def halo_slot(s):
        return s if s < HALO else ROWS + s

    def plane(k, r, tiles):
        return [planes[k, i, pl.ds(r, 8, stride=0), :] for i in tiles]

    def wide(k, r):
        return jnp.concatenate(plane(k, r, (0, 1)), axis=1)

    own, side = 8 * ROWS, 8 * HALO
    edges = [own_table(i) for i in range(PACK)]
    for pack in range(PACKS):
        at = pack * (own + 2 * side)

        def received(start, rows):
            return from_east[start : start + rows, :].astype(F32) + from_west[
                start : start + rows, :
            ].astype(F32)

        x = received(at, own)
        for i in range(PACK):
            x = x + dot(group_rows(p_ref, pack, i), edges[i])
        x = x.reshape(8, ROWS, 128)
        for t in range(ROWS // 8):
            tile = turn(x[:, 8 * t : 8 * t + 8])
            for s in range(8):
                r = HALO + 8 * t + s
                pert_edge[8 * t + s, pack] = tile[s]
                a_edge[r, pack] = tile[s] * plane(GRAD, r, (2,))[0]
        x = [received(at + own + j * side, side) for j in range(2)]
        for j, src in enumerate((from_north, from_south)):
            for i in range(PACK):
                x[j] = x[j] + dot(pack_rows(src, pack, i), edges[i])
        tile = turn(halves(*x))
        for s in range(8):
            r = halo_slot(s)
            a_edge[r, pack] = tile[s] * plane(GRAD, r, (2,))[0]

    def products(n, carry):
        for r in range(ROWS):
            a_ref[HALO + r, n] = pert_ref[n, r] * wide(GRAD, HALO + r)
        here = pl.ds(pl.multiple_of(n * side, side), side)
        tile = turn(halves(*(dot(x[here, :], split[...]) for x in (from_north, from_south))))
        for s in range(8):
            r = halo_slot(s)
            a_ref[r, n] = tile[s] * wide(GRAD, r)
        return carry

    for copy in copies:
        copy.wait()
    lax.fori_loop(0, GROUPS, products, 0)

    def weighted(coefs, x, above, below, left, right):
        out = coefs[0] * x + coefs[1] * above
        out = out + coefs[2] * below
        return (out + coefs[3] * left) + coefs[4] * right

    def stencil(ref, r, n, coefs):
        x = [ref[r, n, :, 128 * i : 128 * i + 128] for i in range(2)]
        left, right = shifted(*x)
        return [
            weighted(
                [c[i] for c in coefs],
                x[i],
                ref[r - 1, n, :, 128 * i : 128 * i + 128],
                ref[r + 1, n, :, 128 * i : 128 * i + 128],
                left[i],
                right[i],
            )
            for i in range(2)
        ]

    def stencil_edge(ref, r, n, coefs):
        x = ref[r, n]
        return weighted([c[2] for c in coefs], x, ref[r - 1, n], ref[r + 1, n], *shifted_edge(x))

    STEP = 4

    def each_row(margin, order, use):
        def rows(first, count):
            for r in range(count):
                use(first + r, [plane(k, first + r, range(3)) for k in order])

        def step(i, carry):
            rows(HALO - margin + STEP * i, STEP)
            return carry

        steps, rest = divmod(ROWS + 2 * margin, STEP)
        lax.fori_loop(0, steps, step, 0)
        rows(HALO - margin + STEP * steps, rest)

    def filter_pass(src, src_edge, dst, dst_edge, margin, order):
        def use(r, coefs):
            for n in range(GROUPS):
                for i, x in enumerate(stencil(src, r, n, coefs)):
                    dst[r, n, :, 128 * i : 128 * i + 128] = x
            for pack in range(PACKS):
                dst_edge[r, pack] = stencil_edge(src_edge, r, pack, coefs)

        each_row(margin, order, use)

    adjoint, forward = (0, 6, 5, 8, 7), range(5)
    filter_pass(a_ref, a_edge, b_ref, b_edge, 3, adjoint)
    filter_pass(b_ref, b_edge, a_ref, a_edge, 2, adjoint)
    filter_pass(a_ref, a_edge, b_ref, b_edge, 1, forward)

    def last(r, coefs):
        total = [None, None]
        for n in range(GROUPS):
            for i, x in enumerate(stencil(b_ref, r, n, coefs)):
                x = pert_ref[n, r - HALO, :, 128 * i : 128 * i + 128] * x
                total[i] = x if total[i] is None else total[i] + x
        for i in range(2):
            sum_ref[r - HALO, :, 128 * i : 128 * i + 128] = total[i]
        total = None
        for pack in range(PACKS):
            x = pert_edge[r - HALO, pack] * stencil_edge(b_edge, r, pack, coefs)
            total = x if total is None else total + x
        sum_edge[r - HALO] = total

    each_row(0, forward, last)

    def members(ref):
        x = jnp.swapaxes(ref[...], 0, 1)
        total = x[0]
        for j in range(1, 8):
            total = total + x[j]
        return total

    lane = lax.broadcasted_iota(jnp.int32, (ROWS, COLS), 1) % 128
    edge = moved(members(sum_edge), back[...])
    total = jnp.where((lane >= 2) & (lane < 126), members(sum_ref), edge)
    out_ref[0] = moved(total, join[...]) * (1.0 / (MEMBERS - 1))


VMEM = pl.BlockSpec(memory_space=pltpu.VMEM)


def call(kernel, outs, scratch=(), stay=()):
    def run(*args):
        here = pl.BlockSpec(memory_space=pl.ANY)
        return pl.pallas_call(
            kernel,
            out_shape=outs,
            in_specs=[here if i in stay else VMEM for i in range(len(args))],
            out_specs=jax.tree.map(lambda _: VMEM, outs),
            scratch_shapes=list(scratch),
        )(*args)

    return run


def level_kernel(src, dst, held, sems):
    count = src.shape[0]
    first = [pltpu.make_async_copy(src.at[m], held.at[m], sems.at[0, m]) for m in range(count)]
    then = [pltpu.make_async_copy(held.at[m], dst.at[:, m], sems.at[1, m]) for m in range(count)]
    for copy in first:
        copy.start()
    for copy, out in zip(first, then):
        copy.wait()
        out.start()
    for copy in then:
        copy.wait()


def by_level(pert):
    members, levels, *block = pert.shape
    here = pl.BlockSpec(memory_space=pl.ANY)
    return pl.pallas_call(
        level_kernel,
        in_specs=[here],
        out_specs=here,
        out_shape=jax.ShapeDtypeStruct((levels, members, *block), pert.dtype),
        scratch_shapes=[
            pltpu.VMEM(pert.shape, pert.dtype),
            pltpu.SemaphoreType.DMA((2, members)),
        ],
    )(pert)


def near(x):
    return pltpu.with_memory_space_constraint(x, pltpu.VMEM)


def swap(to_low, to_high, axis):
    count = lax.axis_size(axis)
    forward = [(i, i + 1) for i in range(count - 1)]
    backward = [(target, source) for source, target in forward]
    return lax.ppermute(to_high, axis, forward), lax.ppermute(to_low, axis, backward)


def extended(block):
    low, high = swap(block[:, :HALO], block[:, -HALO:], "lat")
    block = jnp.concatenate([low, block, high], axis=1)
    low, high = swap(block[:, :, :HALO], block[:, :, -HALO:], "lon")
    return jnp.concatenate([low, block, high], axis=2)


def body(gradient, perturbations, filter_coef):
    spread, split, back, join = tables()
    shape = jax.ShapeDtypeStruct
    pert = by_level(perturbations)
    pert = lax.all_to_all(pert, "mem", split_axis=0, concat_axis=0, tiled=True)
    pert = near(pert.reshape(MEMBERS, ROWS, COLS))
    planes = call(
        planes_kernel,
        shape((PLANES, WIDE // 128, SLOTS, 128), F32),
        [pltpu.VMEM((6, SLOTS + 16, WIDE), F32)],
    )(extended(jnp.concatenate([filter_coef, gradient], axis=0)), spread)
    out = shape((SIDE, COLS), BF16)
    from_north, from_south = swap(*call(row_kernel, [out, out])(pert), "lat")
    from_north, from_south = near(from_north), near(from_south)
    turned = call(turn_kernel, shape((GROUPS, ROWS, 8, COLS), F32))(pert, split)
    cols = shape((MEMBERS * SLOTS // PACK, 128), BF16)
    to_west, to_east = call(col_kernel, [cols, cols])(pert, from_north, from_south)
    from_west, from_east = swap(to_west, to_east, "lon")
    from_west, from_east = near(from_west), near(from_east)
    return call(
        main_kernel,
        shape((1, ROWS, COLS), F32),
        [
            pltpu.VMEM((SLOTS, GROUPS, 8, COLS), F32),
            pltpu.VMEM((SLOTS, GROUPS, 8, COLS), F32),
            pltpu.VMEM((SLOTS, PACKS, 8, 128), F32),
            pltpu.VMEM((SLOTS, PACKS, 8, 128), F32),
            pltpu.VMEM((GROUPS, ROWS, 8, COLS), F32),
            pltpu.VMEM((ROWS, PACKS, 8, 128), F32),
            pltpu.VMEM((ROWS, 8, COLS), F32),
            pltpu.VMEM((ROWS, 8, 128), F32),
            pltpu.SemaphoreType.DMA((GROUPS,)),
        ],
        {1},
    )(pert, turned, planes, from_north, from_south, from_west, from_east, split, back, join)


def solution(mesh):
    return jax.shard_map(
        body,
        mesh=mesh,
        in_specs=(P("mem", "lat", "lon"), P("mem", None, "lat", "lon"), P(None, "lat", "lon")),
        out_specs=P("mem", "lat", "lon"),
        check_vma=False,
    )
```

```python
import jax
import jax.numpy as jnp
import numpy as np
from jax import lax
from jax.experimental import pallas as pl
from jax.experimental.pallas import tpu as pltpu
from jax.sharding import PartitionSpec as P


MEMBERS = 80
GROUPS = MEMBERS // 8
PACK = 5
PACKS = GROUPS // PACK
ROWS = 32
COLS = 256
HALO = 4
SLOTS = ROWS + 2 * HALO
EDGE = 24
WIDE = COLS + 128
GRAD, PLANES = 9, 10
SIDE = MEMBERS * HALO
F32, BF16 = jnp.float32, jnp.bfloat16


def one_hot(depth, width, pairs):
    table = np.zeros((depth, width), np.float32)
    for source, target in pairs:
        table[source, target] = 1.0
    return table.astype(BF16)


def split_pairs(first=0):
    return [(first + c, c // 2 + 128 * (c % 2)) for c in range(COLS)]


def tables():
    spread, back = [], []
    for i in range(PACK):
        at = EDGE * i
        spread += [(c, COLS + at + c) for c in range(12)]
        spread += [(COLS - 16 + c, COLS + at + c) for c in range(12, 24)]
        back += [(at + 4 + c, c // 2 + 128 * (c % 2)) for c in range(4)]
        back += [(at + 16 + c, 126 + c // 2 + 128 * (c % 2)) for c in range(4)]
    planes = one_hot(COLS + 2 * HALO, WIDE, split_pairs(HALO) + spread)
    join = one_hot(COLS, COLS, [(target, source) for source, target in split_pairs()])
    split = one_hot(COLS, COLS, split_pairs())
    return planes, split, one_hot(128, COLS, back), join


def edge_table(width, first, last, count):
    def ends(shift, keep):
        row = lax.broadcasted_iota(jnp.int32, (16, width), 0)
        lane = lax.broadcasted_iota(jnp.int32, (16, width), 1)
        return jnp.where((lane - row == shift) & keep(row), 1.0, 0.0).astype(BF16)

    top = ends(first, lambda row: row < count)
    bottom = ends(last + count - 16, lambda row: row >= 16 - count)
    return jnp.concatenate([top, jnp.zeros((COLS - 32, width), BF16), bottom], axis=0)


def send_table(i):
    return edge_table(256, EDGE * i + 20, 128 + EDGE * i, 4)


def own_table(i):
    return edge_table(128, EDGE * i + 4, EDGE * i + 12, 8)


def parts(x, count=3):
    out = []
    for _ in range(count):
        out.append(x.astype(BF16))
        x = x - out[-1].astype(F32)
    return out


def dot(a, b):
    return jnp.dot(a, b, preferred_element_type=F32)


def moved(x, table):
    first, second, third = (dot(y, table) for y in parts(x))
    return (third + second) + first


def planes_kernel(x_ref, table, out_ref, rows_ref):
    for k in range(6):
        x = moved(x_ref[k], table[...])
        for i in range(WIDE // 128):
            lanes = slice(128 * i, 128 * i + 128)
            out_ref[(GRAD if k == 5 else k), i] = x[:, lanes]
            rows_ref[k, 8 : 8 + SLOTS, lanes] = x[:, lanes]
    inside = rows_ref[0, 8 : 8 + SLOTS, :] > 0.0
    below = rows_ref[1, 9 : 9 + SLOTS, :]
    above = rows_ref[2, 7 : 7 + SLOTS, :]
    right = both(rows_ref[3, 8 : 8 + SLOTS, :])[1]
    left = both(rows_ref[4, 8 : 8 + SLOTS, :])[0]
    for k, x in enumerate((below, above, right, left)):
        x = jnp.where(inside, x, 0.0)
        for i in range(WIDE // 128):
            out_ref[5 + k, i] = x[:, 128 * i : 128 * i + 128]


def shifted(even, odd):
    left = (pltpu.roll(odd, 1, 1), even)
    right = (odd, pltpu.roll(even, 127, 1))
    return left, right


def shifted_edge(x):
    return pltpu.roll(x, 1, 1), pltpu.roll(x, 127, 1)


def both(x):
    left, right = shifted(x[:, :128], x[:, 128:256])
    edge_left, edge_right = shifted_edge(x[:, 256:])
    return jnp.concatenate([*left, edge_left], 1), jnp.concatenate([*right, edge_right], 1)


def row_kernel(p_ref, north_ref, south_ref):
    low = lax.broadcasted_iota(jnp.int32, (8, COLS), 0) < HALO
    for q in range(0, MEMBERS, 4):
        x = [p_ref[q + i, :8].astype(F32) for i in range(4)]
        x = [jnp.where(low, x[i], pltpu.roll(x[i + 1], 4, 0)) for i in (0, 2)]
        north_ref[4 * q : 4 * q + 16, :] = jnp.concatenate(x, axis=0).astype(BF16)
        x = [p_ref[q + i, ROWS - 8 :].astype(F32) for i in range(4)]
        x = [jnp.where(low, pltpu.roll(x[i], 4, 0), x[i + 1]) for i in (0, 2)]
        south_ref[4 * q : 4 * q + 16, :] = jnp.concatenate(x, axis=0).astype(BF16)


def pack_rows(ref, pack, i):
    size = 8 * HALO
    return ref[pl.ds((PACK * pack + i) * size, size), :]


def group_rows(ref, pack, i):
    return ref[pl.ds(8 * (PACK * pack + i), 8)].reshape(8 * ROWS, COLS)


def col_kernel(p_ref, from_north, from_south, west_ref, east_ref):
    send = [send_table(i) for i in range(PACK)]
    own, side = 8 * ROWS, 8 * HALO
    edges = [own_table(i) for i in range(PACK)]
    for pack in range(PACKS):
        at = pack * (own + 2 * side)
        for rows, get in (
            (own, lambda i: group_rows(p_ref, pack, i)),
            (side, lambda i: pack_rows(from_north, pack, i)),
            (side, lambda i: pack_rows(from_south, pack, i)),
        ):
            x = dot(get(0), send[0])
            for i in range(1, PACK):
                x = x + dot(get(i), send[i])
            west_ref[at : at + rows, :] = x[:, :128].astype(BF16)
            east_ref[at : at + rows, :] = x[:, 128:].astype(BF16)
            at += rows


def turn(tile):
    return jnp.swapaxes(tile, 0, 1)


def turn_kernel(p_ref, split, out_ref, edge_ref):
    edges = [own_table(i) for i in range(PACK)]
    for pack in range(PACKS):
        x = dot(group_rows(p_ref, pack, 0), edges[0])
        for i in range(1, PACK):
            x = x + dot(group_rows(p_ref, pack, i), edges[i])
        edge_ref[pack] = x.astype(BF16)

    def group(n, carry):
        x = p_ref[pl.ds(pl.multiple_of(8 * n, 8), 8)].reshape(8 * ROWS, COLS)
        x = dot(x, split[...]).reshape(8, ROWS, COLS)
        for t in range(ROWS // 8):
            tile = turn(x[:, 8 * t : 8 * t + 8])
            for s in range(8):
                out_ref[n, 8 * t + s] = tile[s]
        return carry

    lax.fori_loop(0, GROUPS, group, 0)


def halves(north, south):
    low = lax.broadcasted_iota(jnp.int32, (8, north.shape[1]), 0) < HALO
    tiles = []
    for q in range(north.shape[0] // 8):
        n, s = north[8 * q : 8 * q + 8], south[8 * q : 8 * q + 8]
        tiles.append(jnp.where(low, n, pltpu.roll(s, 4, 0)))
        tiles.append(jnp.where(low, pltpu.roll(n, 4, 0), s))
    return jnp.stack(tiles)


def halo_slot(s):
    return s if s < HALO else ROWS + s


def row_of(planes, k, r, tiles):
    return [planes[k, i, pl.ds(r, 8, stride=0), :] for i in tiles]


def weighted(coefs, x, above, below, left, right):
    out = coefs[0] * x + coefs[1] * above
    out = out + coefs[2] * below
    return (out + coefs[3] * left) + coefs[4] * right


def each_row(margin, stride, use):
    def rows(first, count):
        for r in range(count):
            use(first + r)

    def step(i, carry):
        rows(HALO - margin + stride * i, stride)
        return carry

    steps, rest = divmod(ROWS + 2 * margin, stride)
    lax.fori_loop(0, steps, step, 0)
    rows(HALO - margin + stride * steps, rest)


def members(ref):
    x = jnp.swapaxes(ref[...], 0, 1)
    total = x[0]
    for j in range(1, 8):
        total = total + x[j]
    return total


ADJOINT, FORWARD = (0, 6, 5, 8, 7), range(5)
OWN_ROWS, SIDE_ROWS = 8 * ROWS, 8 * HALO


def main_kernel(
    own_edge, turned, planes, from_north, from_south, split, out_ref, edge_ref,
    a_ref, b_ref, pert_ref, sum_ref, sems,
):
    copies = [
        pltpu.make_async_copy(turned.at[n], pert_ref.at[n], sems.at[n]) for n in range(GROUPS)
    ]
    for copy in copies:
        copy.start()

    edges = [own_table(i) for i in range(PACK)]
    for pack in range(PACKS):
        at = pack * (OWN_ROWS + 2 * SIDE_ROWS)
        edge_ref[at : at + OWN_ROWS, :] = own_edge[pack]
        at += OWN_ROWS
        for src in (from_north, from_south):
            x = dot(pack_rows(src, pack, 0), edges[0])
            for i in range(1, PACK):
                x = x + dot(pack_rows(src, pack, i), edges[i])
            edge_ref[at : at + SIDE_ROWS, :] = x.astype(BF16)
            at += SIDE_ROWS

    def wide(k, r):
        return jnp.concatenate(row_of(planes, k, r, (0, 1)), axis=1)

    def products(n, carry):
        for r in range(ROWS):
            a_ref[HALO + r, n] = pert_ref[n, r] * wide(GRAD, HALO + r)
        here = pl.ds(pl.multiple_of(n * SIDE_ROWS, SIDE_ROWS), SIDE_ROWS)
        tile = turn(halves(*(dot(x[here, :], split[...]) for x in (from_north, from_south))))
        for s in range(8):
            r = halo_slot(s)
            a_ref[r, n] = tile[s] * wide(GRAD, r)
        return carry

    for copy in copies:
        copy.wait()
    lax.fori_loop(0, GROUPS, products, 0)

    def stencil(ref, r, n, coefs):
        x = [ref[r, n, :, 128 * i : 128 * i + 128] for i in range(2)]
        left, right = shifted(*x)
        return [
            weighted(
                [c[i] for c in coefs],
                x[i],
                ref[r - 1, n, :, 128 * i : 128 * i + 128],
                ref[r + 1, n, :, 128 * i : 128 * i + 128],
                left[i],
                right[i],
            )
            for i in range(2)
        ]

    def filter_pass(src, dst, margin, order):
        def use(r):
            coefs = [row_of(planes, k, r, range(2)) for k in order]
            for n in range(GROUPS):
                for i, x in enumerate(stencil(src, r, n, coefs)):
                    dst[r, n, :, 128 * i : 128 * i + 128] = x

        each_row(margin, 6, use)

    filter_pass(a_ref, b_ref, 3, ADJOINT)
    filter_pass(b_ref, a_ref, 2, ADJOINT)
    filter_pass(a_ref, b_ref, 1, FORWARD)

    def last(r):
        coefs = [row_of(planes, k, r, range(2)) for k in FORWARD]
        total = [None, None]
        for n in range(GROUPS):
            for i, x in enumerate(stencil(b_ref, r, n, coefs)):
                x = pert_ref[n, r - HALO, :, 128 * i : 128 * i + 128] * x
                total[i] = x if total[i] is None else total[i] + x
        for i in range(2):
            sum_ref[r - HALO, :, 128 * i : 128 * i + 128] = total[i]

    each_row(0, 6, last)
    out_ref[...] = members(sum_ref)


def edge_kernel(
    main, edge, planes, from_west, from_east, back, join, out_ref, a_ref, b_ref, pert_ref, sum_ref
):
    for pack in range(PACKS):
        at = pack * (OWN_ROWS + 2 * SIDE_ROWS)

        def whole(start, rows):
            return sum(x[start : start + rows, :].astype(F32) for x in (edge, from_west, from_east))

        x = whole(at, OWN_ROWS).reshape(8, ROWS, 128)
        for t in range(ROWS // 8):
            tile = turn(x[:, 8 * t : 8 * t + 8])
            for s in range(8):
                r = HALO + 8 * t + s
                pert_ref[8 * t + s, pack] = tile[s]
                a_ref[r, pack] = tile[s] * row_of(planes, GRAD, r, (2,))[0]
        x = (whole(at + OWN_ROWS + j * SIDE_ROWS, SIDE_ROWS) for j in range(2))
        tile = turn(halves(*x))
        for s in range(8):
            r = halo_slot(s)
            a_ref[r, pack] = tile[s] * row_of(planes, GRAD, r, (2,))[0]

    def stencil(ref, r, pack, coefs):
        x = ref[r, pack]
        return weighted(coefs, x, ref[r - 1, pack], ref[r + 1, pack], *shifted_edge(x))

    def filter_pass(src, dst, margin, order):
        def use(r):
            coefs = [row_of(planes, k, r, (2,))[0] for k in order]
            for pack in range(PACKS):
                dst[r, pack] = stencil(src, r, pack, coefs)

        each_row(margin, 8, use)

    filter_pass(a_ref, b_ref, 3, ADJOINT)
    filter_pass(b_ref, a_ref, 2, ADJOINT)
    filter_pass(a_ref, b_ref, 1, FORWARD)

    def last(r):
        coefs = [row_of(planes, k, r, (2,))[0] for k in FORWARD]
        total = None
        for pack in range(PACKS):
            x = pert_ref[r - HALO, pack] * stencil(b_ref, r, pack, coefs)
            total = x if total is None else total + x
        sum_ref[r - HALO] = total

    each_row(0, 8, last)
    lane = lax.broadcasted_iota(jnp.int32, (ROWS, COLS), 1) % 128
    x = moved(members(sum_ref), back[...])
    total = jnp.where((lane >= 2) & (lane < 126), main[...], x)
    out_ref[0] = moved(total, join[...]) * (1.0 / (MEMBERS - 1))


VMEM = pl.BlockSpec(memory_space=pltpu.VMEM)


def call(kernel, outs, scratch=(), stay=()):
    def run(*args):
        here = pl.BlockSpec(memory_space=pl.ANY)
        return pl.pallas_call(
            kernel,
            out_shape=outs,
            in_specs=[here if i in stay else VMEM for i in range(len(args))],
            out_specs=jax.tree.map(lambda _: VMEM, outs),
            scratch_shapes=list(scratch),
        )(*args)

    return run


def level_kernel(src, dst, held, sems):
    count = src.shape[0]
    first = [pltpu.make_async_copy(src.at[m], held.at[m], sems.at[0, m]) for m in range(count)]
    then = [pltpu.make_async_copy(held.at[m], dst.at[:, m], sems.at[1, m]) for m in range(count)]
    for copy in first:
        copy.start()
    for copy, out in zip(first, then):
        copy.wait()
        out.start()
    for copy in then:
        copy.wait()


def by_level(pert):
    members, levels, *block = pert.shape
    here = pl.BlockSpec(memory_space=pl.ANY)
    return pl.pallas_call(
        level_kernel,
        in_specs=[here],
        out_specs=here,
        out_shape=jax.ShapeDtypeStruct((levels, members, *block), pert.dtype),
        scratch_shapes=[
            pltpu.VMEM(pert.shape, pert.dtype),
            pltpu.SemaphoreType.DMA((2, members)),
        ],
    )(pert)


def near(x):
    return pltpu.with_memory_space_constraint(x, pltpu.VMEM)


def swap(to_low, to_high, axis):
    count = lax.axis_size(axis)
    forward = [(i, i + 1) for i in range(count - 1)]
    backward = [(target, source) for source, target in forward]
    return lax.ppermute(to_high, axis, forward), lax.ppermute(to_low, axis, backward)


def extended(block):
    low, high = swap(block[:, :HALO], block[:, -HALO:], "lat")
    block = jnp.concatenate([low, block, high], axis=1)
    low, high = swap(block[:, :, :HALO], block[:, :, -HALO:], "lon")
    return jnp.concatenate([low, block, high], axis=2)


def body(gradient, perturbations, filter_coef):
    spread, split, back, join = tables()
    shape = jax.ShapeDtypeStruct
    pert = by_level(perturbations)
    pert = lax.all_to_all(pert, "mem", split_axis=0, concat_axis=0, tiled=True)
    pert = near(pert.reshape(MEMBERS, ROWS, COLS))
    planes = call(
        planes_kernel,
        shape((PLANES, WIDE // 128, SLOTS, 128), F32),
        [pltpu.VMEM((6, SLOTS + 16, WIDE), F32)],
    )(extended(jnp.concatenate([filter_coef, gradient], axis=0)), spread)
    out = shape((SIDE, COLS), BF16)
    from_north, from_south = swap(*call(row_kernel, [out, out])(pert), "lat")
    from_north, from_south = near(from_north), near(from_south)
    turned, own_edge = call(
        turn_kernel,
        [shape((GROUPS, ROWS, 8, COLS), F32), shape((PACKS, OWN_ROWS, 128), BF16)],
    )(pert, split)
    cols = shape((MEMBERS * SLOTS // PACK, 128), BF16)
    to_west, to_east = call(col_kernel, [cols, cols])(pert, from_north, from_south)
    from_west, from_east = swap(to_west, to_east, "lon")
    from_west, from_east = near(from_west), near(from_east)
    main, edge = call(
        main_kernel,
        [shape((ROWS, COLS), F32), cols],
        [
            pltpu.VMEM((SLOTS, GROUPS, 8, COLS), F32),
            pltpu.VMEM((SLOTS, GROUPS, 8, COLS), F32),
            pltpu.VMEM((GROUPS, ROWS, 8, COLS), F32),
            pltpu.VMEM((ROWS, 8, COLS), F32),
            pltpu.SemaphoreType.DMA((GROUPS,)),
        ],
        {1},
    )(own_edge, turned, planes, from_north, from_south, split)
    return call(
        edge_kernel,
        shape((1, ROWS, COLS), F32),
        [
            pltpu.VMEM((SLOTS, PACKS, 8, 128), F32),
            pltpu.VMEM((SLOTS, PACKS, 8, 128), F32),
            pltpu.VMEM((ROWS, PACKS, 8, 128), F32),
            pltpu.VMEM((ROWS, 8, 128), F32),
        ],
    )(main, edge, planes, from_west, from_east, back, join)


def solution(mesh):
    return jax.shard_map(
        body,
        mesh=mesh,
        in_specs=(P("mem", "lat", "lon"), P("mem", None, "lat", "lon"), P(None, "lat", "lon")),
        out_specs=P("mem", "lat", "lon"),
        check_vma=False,
    )
```

```python
import jax
import jax.numpy as jnp
import numpy as np
from jax import lax
from jax.experimental import pallas as pl
from jax.experimental.pallas import tpu as pltpu
from jax.sharding import PartitionSpec as P


MEMBERS = 80
GROUPS = MEMBERS // 8
PACK = 5
PACKS = GROUPS // PACK
ROWS = 32
COLS = 256
HALO = 4
SLOTS = ROWS + 2 * HALO
EDGE = 24
WIDE = COLS + 128
GRAD, PLANES = 9, 10
SIDE = MEMBERS * HALO
F32, BF16 = jnp.float32, jnp.bfloat16


def one_hot(depth, width, pairs):
    table = np.zeros((depth, width), np.float32)
    for source, target in pairs:
        table[source, target] = 1.0
    return table.astype(BF16)


def split_pairs(first=0):
    return [(first + c, c // 2 + 128 * (c % 2)) for c in range(COLS)]


def tables():
    spread, back = [], []
    for i in range(PACK):
        at = EDGE * i
        spread += [(c, COLS + at + c) for c in range(12)]
        spread += [(COLS - 16 + c, COLS + at + c) for c in range(12, 24)]
        back += [(at + 4 + c, c // 2 + 128 * (c % 2)) for c in range(4)]
        back += [(at + 16 + c, 126 + c // 2 + 128 * (c % 2)) for c in range(4)]
    planes = one_hot(COLS + 2 * HALO, WIDE, split_pairs(HALO) + spread)
    join = one_hot(COLS, COLS, [(target, source) for source, target in split_pairs()])
    split = one_hot(COLS, COLS, split_pairs())
    return planes, split, one_hot(128, COLS, back), join


def edge_table(width, first, last, count):
    def ends(shift, keep):
        row = lax.broadcasted_iota(jnp.int32, (16, width), 0)
        lane = lax.broadcasted_iota(jnp.int32, (16, width), 1)
        return jnp.where((lane - row == shift) & keep(row), 1.0, 0.0).astype(BF16)

    top = ends(first, lambda row: row < count)
    bottom = ends(last + count - 16, lambda row: row >= 16 - count)
    return jnp.concatenate([top, jnp.zeros((COLS - 32, width), BF16), bottom], axis=0)


def send_table(i):
    return edge_table(256, EDGE * i + 20, 128 + EDGE * i, 4)


def own_table(i):
    return edge_table(128, EDGE * i + 4, EDGE * i + 12, 8)


def parts(x, count=3):
    out = []
    for _ in range(count):
        out.append(x.astype(BF16))
        x = x - out[-1].astype(F32)
    return out


def dot(a, b):
    return jnp.dot(a, b, preferred_element_type=F32)


def moved(x, table):
    first, second, third = (dot(y, table) for y in parts(x))
    return (third + second) + first


def planes_kernel(x_ref, table, out_ref, rows_ref):
    for k in range(6):
        x = moved(x_ref[k], table[...])
        for i in range(WIDE // 128):
            lanes = slice(128 * i, 128 * i + 128)
            out_ref[(GRAD if k == 5 else k), i] = x[:, lanes]
            rows_ref[k, 8 : 8 + SLOTS, lanes] = x[:, lanes]
    inside = rows_ref[0, 8 : 8 + SLOTS, :] > 0.0
    below = rows_ref[1, 9 : 9 + SLOTS, :]
    above = rows_ref[2, 7 : 7 + SLOTS, :]
    right = both(rows_ref[3, 8 : 8 + SLOTS, :])[1]
    left = both(rows_ref[4, 8 : 8 + SLOTS, :])[0]
    for k, x in enumerate((below, above, right, left)):
        x = jnp.where(inside, x, 0.0)
        for i in range(WIDE // 128):
            out_ref[5 + k, i] = x[:, 128 * i : 128 * i + 128]


def shifted(even, odd):
    left = (pltpu.roll(odd, 1, 1), even)
    right = (odd, pltpu.roll(even, 127, 1))
    return left, right


def shifted_edge(x):
    return pltpu.roll(x, 1, 1), pltpu.roll(x, 127, 1)


def both(x):
    left, right = shifted(x[:, :128], x[:, 128:256])
    edge_left, edge_right = shifted_edge(x[:, 256:])
    return jnp.concatenate([*left, edge_left], 1), jnp.concatenate([*right, edge_right], 1)


def row_kernel(p_ref, north_ref, south_ref):
    low = lax.broadcasted_iota(jnp.int32, (8, COLS), 0) < HALO
    for q in range(0, MEMBERS, 4):
        x = [p_ref[q + i, :8].astype(F32) for i in range(4)]
        x = [jnp.where(low, x[i], pltpu.roll(x[i + 1], 4, 0)) for i in (0, 2)]
        north_ref[4 * q : 4 * q + 16, :] = jnp.concatenate(x, axis=0).astype(BF16)
        x = [p_ref[q + i, ROWS - 8 :].astype(F32) for i in range(4)]
        x = [jnp.where(low, pltpu.roll(x[i], 4, 0), x[i + 1]) for i in (0, 2)]
        south_ref[4 * q : 4 * q + 16, :] = jnp.concatenate(x, axis=0).astype(BF16)


def pack_rows(ref, pack, i):
    size = 8 * HALO
    return ref[pl.ds((PACK * pack + i) * size, size), :]


def group_rows(ref, pack, i):
    return ref[pl.ds(8 * (PACK * pack + i), 8)].reshape(8 * ROWS, COLS)


def col_kernel(p_ref, from_north, from_south, west_ref, east_ref):
    send = [send_table(i) for i in range(PACK)]
    own, side = 8 * ROWS, 8 * HALO
    edges = [own_table(i) for i in range(PACK)]
    for pack in range(PACKS):
        at = pack * (own + 2 * side)
        for rows, get in (
            (own, lambda i: group_rows(p_ref, pack, i)),
            (side, lambda i: pack_rows(from_north, pack, i)),
            (side, lambda i: pack_rows(from_south, pack, i)),
        ):
            x = dot(get(0), send[0])
            for i in range(1, PACK):
                x = x + dot(get(i), send[i])
            west_ref[at : at + rows, :] = x[:, :128].astype(BF16)
            east_ref[at : at + rows, :] = x[:, 128:].astype(BF16)
            at += rows


def turn(tile):
    return jnp.swapaxes(tile, 0, 1)


def turn_kernel(p_ref, split, out_ref, edge_ref):
    edges = [own_table(i) for i in range(PACK)]
    for pack in range(PACKS):
        x = dot(group_rows(p_ref, pack, 0), edges[0])
        for i in range(1, PACK):
            x = x + dot(group_rows(p_ref, pack, i), edges[i])
        edge_ref[pack] = x.astype(BF16)

    def group(n, carry):
        x = p_ref[pl.ds(pl.multiple_of(8 * n, 8), 8)].reshape(8 * ROWS, COLS)
        x = dot(x, split[...]).reshape(8, ROWS, COLS)
        for t in range(ROWS // 8):
            tile = turn(x[:, 8 * t : 8 * t + 8])
            for s in range(8):
                out_ref[n, 8 * t + s] = tile[s]
        return carry

    lax.fori_loop(0, GROUPS, group, 0)


def halves(north, south):
    low = lax.broadcasted_iota(jnp.int32, (8, north.shape[1]), 0) < HALO
    tiles = []
    for q in range(north.shape[0] // 8):
        n, s = north[8 * q : 8 * q + 8], south[8 * q : 8 * q + 8]
        tiles.append(jnp.where(low, n, pltpu.roll(s, 4, 0)))
        tiles.append(jnp.where(low, pltpu.roll(n, 4, 0), s))
    return jnp.stack(tiles)


def halo_slot(s):
    return s if s < HALO else ROWS + s


def row_of(planes, k, r, tiles):
    return [planes[k, i, pl.ds(r, 8, stride=0), :] for i in tiles]


def weighted(coefs, x, above, below, left, right):
    out = coefs[0] * x + coefs[1] * above
    out = out + coefs[2] * below
    return (out + coefs[3] * left) + coefs[4] * right


def each_row(margin, stride, use):
    def rows(first, count):
        for r in range(count):
            use(first + r)

    def step(i, carry):
        rows(HALO - margin + stride * i, stride)
        return carry

    steps, rest = divmod(ROWS + 2 * margin, stride)
    lax.fori_loop(0, steps, step, 0)
    rows(HALO - margin + stride * steps, rest)


def members(ref):
    x = jnp.swapaxes(ref[...], 0, 1)
    total = x[0]
    for j in range(1, 8):
        total = total + x[j]
    return total


ADJOINT, FORWARD = (0, 6, 5, 8, 7), range(5)
OWN_ROWS, SIDE_ROWS = 8 * ROWS, 8 * HALO


def main_kernel(
    own_edge, turned, planes, from_north, from_south, split, out_ref, edge_ref,
    a_ref, b_ref, pert_ref, sum_ref, sems,
):
    copies = [
        pltpu.make_async_copy(turned.at[n], pert_ref.at[n], sems.at[n]) for n in range(GROUPS)
    ]
    for copy in copies:
        copy.start()

    edges = [own_table(i) for i in range(PACK)]
    for pack in range(PACKS):
        at = pack * (OWN_ROWS + 2 * SIDE_ROWS)
        edge_ref[at : at + OWN_ROWS, :] = own_edge[pack]
        at += OWN_ROWS
        for src in (from_north, from_south):
            x = dot(pack_rows(src, pack, 0), edges[0])
            for i in range(1, PACK):
                x = x + dot(pack_rows(src, pack, i), edges[i])
            edge_ref[at : at + SIDE_ROWS, :] = x.astype(BF16)
            at += SIDE_ROWS

    def wide(k, r):
        return jnp.concatenate(row_of(planes, k, r, (0, 1)), axis=1)

    def products(n, carry):
        for r in range(ROWS):
            a_ref[HALO + r, n] = pert_ref[n, r] * wide(GRAD, HALO + r)
        here = pl.ds(pl.multiple_of(n * SIDE_ROWS, SIDE_ROWS), SIDE_ROWS)
        tile = turn(halves(*(dot(x[here, :], split[...]) for x in (from_north, from_south))))
        for s in range(8):
            r = halo_slot(s)
            a_ref[r, n] = tile[s] * wide(GRAD, r)
        return carry

    for copy in copies:
        copy.wait()
    lax.fori_loop(0, GROUPS, products, 0)

    def stencil(ref, r, n, coefs):
        x = [ref[r, n, :, 128 * i : 128 * i + 128] for i in range(2)]
        left, right = shifted(*x)
        return [
            weighted(
                [c[i] for c in coefs],
                x[i],
                ref[r - 1, n, :, 128 * i : 128 * i + 128],
                ref[r + 1, n, :, 128 * i : 128 * i + 128],
                left[i],
                right[i],
            )
            for i in range(2)
        ]

    def filter_pass(src, dst, margin, order):
        def use(r):
            coefs = [row_of(planes, k, r, range(2)) for k in order]
            for n in range(GROUPS):
                for i, x in enumerate(stencil(src, r, n, coefs)):
                    dst[r, n, :, 128 * i : 128 * i + 128] = x

        each_row(margin, 6, use)

    filter_pass(a_ref, b_ref, 3, ADJOINT)
    filter_pass(b_ref, a_ref, 2, ADJOINT)
    filter_pass(a_ref, b_ref, 1, FORWARD)

    def last(r):
        coefs = [row_of(planes, k, r, range(2)) for k in FORWARD]
        total = [None, None]
        for n in range(GROUPS):
            for i, x in enumerate(stencil(b_ref, r, n, coefs)):
                x = pert_ref[n, r - HALO, :, 128 * i : 128 * i + 128] * x
                total[i] = x if total[i] is None else total[i] + x
        for i in range(2):
            sum_ref[r - HALO, :, 128 * i : 128 * i + 128] = total[i]

    each_row(0, 6, last)
    out_ref[...] = members(sum_ref)


def edge_kernel(
    main, edge, planes, from_west, from_east, back, join, out_ref, a_ref, b_ref, pert_ref, sum_ref
):
    for pack in range(PACKS):
        at = pack * (OWN_ROWS + 2 * SIDE_ROWS)

        def whole(start, rows):
            return sum(x[start : start + rows, :].astype(F32) for x in (edge, from_west, from_east))

        x = whole(at, OWN_ROWS).reshape(8, ROWS, 128)
        for t in range(ROWS // 8):
            tile = turn(x[:, 8 * t : 8 * t + 8])
            for s in range(8):
                r = HALO + 8 * t + s
                pert_ref[8 * t + s, pack] = tile[s]
                a_ref[r, pack] = tile[s] * row_of(planes, GRAD, r, (2,))[0]
        x = (whole(at + OWN_ROWS + j * SIDE_ROWS, SIDE_ROWS) for j in range(2))
        tile = turn(halves(*x))
        for s in range(8):
            r = halo_slot(s)
            a_ref[r, pack] = tile[s] * row_of(planes, GRAD, r, (2,))[0]

    def stencil(ref, r, pack, coefs):
        x = ref[r, pack]
        return weighted(coefs, x, ref[r - 1, pack], ref[r + 1, pack], *shifted_edge(x))

    def filter_pass(src, dst, margin, order):
        def use(r):
            coefs = [row_of(planes, k, r, (2,))[0] for k in order]
            for pack in range(PACKS):
                dst[r, pack] = stencil(src, r, pack, coefs)

        each_row(margin, 12, use)

    filter_pass(a_ref, b_ref, 3, ADJOINT)
    filter_pass(b_ref, a_ref, 2, ADJOINT)
    filter_pass(a_ref, b_ref, 1, FORWARD)

    def last(r):
        coefs = [row_of(planes, k, r, (2,))[0] for k in FORWARD]
        total = None
        for pack in range(PACKS):
            x = pert_ref[r - HALO, pack] * stencil(b_ref, r, pack, coefs)
            total = x if total is None else total + x
        sum_ref[r - HALO] = total

    each_row(0, 12, last)
    lane = lax.broadcasted_iota(jnp.int32, (ROWS, COLS), 1) % 128
    x = moved(members(sum_ref), back[...])
    total = jnp.where((lane >= 2) & (lane < 126), main[...], x)
    out_ref[0] = moved(total, join[...]) * (1.0 / (MEMBERS - 1))


VMEM = pl.BlockSpec(memory_space=pltpu.VMEM)


def call(kernel, outs, scratch=(), stay=()):
    def run(*args):
        here = pl.BlockSpec(memory_space=pl.ANY)
        return pl.pallas_call(
            kernel,
            out_shape=outs,
            in_specs=[here if i in stay else VMEM for i in range(len(args))],
            out_specs=jax.tree.map(lambda _: VMEM, outs),
            scratch_shapes=list(scratch),
        )(*args)

    return run


def level_kernel(src, dst, held, sems):
    count = src.shape[0]
    first = [pltpu.make_async_copy(src.at[m], held.at[m], sems.at[0, m]) for m in range(count)]
    then = [pltpu.make_async_copy(held.at[m], dst.at[:, m], sems.at[1, m]) for m in range(count)]
    for copy in first:
        copy.start()
    for copy, out in zip(first, then):
        copy.wait()
        out.start()
    for copy in then:
        copy.wait()


def by_level(pert):
    members, levels, *block = pert.shape
    here = pl.BlockSpec(memory_space=pl.ANY)
    return pl.pallas_call(
        level_kernel,
        in_specs=[here],
        out_specs=here,
        out_shape=jax.ShapeDtypeStruct((levels, members, *block), pert.dtype),
        scratch_shapes=[
            pltpu.VMEM(pert.shape, pert.dtype),
            pltpu.SemaphoreType.DMA((2, members)),
        ],
    )(pert)


def near(x):
    return pltpu.with_memory_space_constraint(x, pltpu.VMEM)


def swap(to_low, to_high, axis):
    count = lax.axis_size(axis)
    forward = [(i, i + 1) for i in range(count - 1)]
    backward = [(target, source) for source, target in forward]
    return lax.ppermute(to_high, axis, forward), lax.ppermute(to_low, axis, backward)


def extended(block):
    low, high = swap(block[:, :HALO], block[:, -HALO:], "lat")
    block = jnp.concatenate([low, block, high], axis=1)
    low, high = swap(block[:, :, :HALO], block[:, :, -HALO:], "lon")
    return jnp.concatenate([low, block, high], axis=2)


def body(gradient, perturbations, filter_coef):
    spread, split, back, join = tables()
    shape = jax.ShapeDtypeStruct
    pert = by_level(perturbations)
    pert = lax.all_to_all(pert, "mem", split_axis=0, concat_axis=0, tiled=True)
    pert = near(pert.reshape(MEMBERS, ROWS, COLS))
    planes = call(
        planes_kernel,
        shape((PLANES, WIDE // 128, SLOTS, 128), F32),
        [pltpu.VMEM((6, SLOTS + 16, WIDE), F32)],
    )(extended(jnp.concatenate([filter_coef, gradient], axis=0)), spread)
    planes = near(planes)
    out = shape((SIDE, COLS), BF16)
    from_north, from_south = swap(*call(row_kernel, [out, out])(pert), "lat")
    from_north, from_south = near(from_north), near(from_south)
    turned, own_edge = call(
        turn_kernel,
        [shape((GROUPS, ROWS, 8, COLS), F32), shape((PACKS, OWN_ROWS, 128), BF16)],
    )(pert, split)
    cols = shape((MEMBERS * SLOTS // PACK, 128), BF16)
    to_west, to_east = call(col_kernel, [cols, cols])(pert, from_north, from_south)
    from_west, from_east = swap(to_west, to_east, "lon")
    from_west, from_east = near(from_west), near(from_east)
    main, edge = call(
        main_kernel,
        [shape((ROWS, COLS), F32), cols],
        [
            pltpu.VMEM((SLOTS, GROUPS, 8, COLS), F32),
            pltpu.VMEM((SLOTS, GROUPS, 8, COLS), F32),
            pltpu.VMEM((GROUPS, ROWS, 8, COLS), F32),
            pltpu.VMEM((ROWS, 8, COLS), F32),
            pltpu.SemaphoreType.DMA((GROUPS,)),
        ],
        {1},
    )(own_edge, turned, planes, from_north, from_south, split)
    return call(
        edge_kernel,
        shape((1, ROWS, COLS), F32),
        [
            pltpu.VMEM((SLOTS, PACKS, 8, 128), F32),
            pltpu.VMEM((SLOTS, PACKS, 8, 128), F32),
            pltpu.VMEM((ROWS, PACKS, 8, 128), F32),
            pltpu.VMEM((ROWS, 8, 128), F32),
        ],
    )(main, edge, planes, from_west, from_east, back, join)


def solution(mesh):
    return jax.shard_map(
        body,
        mesh=mesh,
        in_specs=(P("mem", "lat", "lon"), P("mem", None, "lat", "lon"), P(None, "lat", "lon")),
        out_specs=P("mem", "lat", "lon"),
        check_vma=False,
    )
```
